512 devices in a mesh: seq: 64 (over x, y, core), head: 8 (over z).
Axes of the slice: x: 4, y: 8, z: 8, core: 2. Of those that a mesh axis runs over, the one named last changes fastest.
Arguments:
- query_rows: bfloat16 [8192, 3072], P(('seq', 'head')), may hold values from -5 to 5
- key_rows: bfloat16 [8192, 3072], P(('seq', 'head')), may hold values from -5 to 5
- value_rows: bfloat16 [8192, 3072], P(('seq', 'head')), may hold values from -6 to 6
- out_grad: bfloat16 [8192, 3072], P(('seq', 'head')), may hold values from -6 to 6
- block_mask: int32 [4, 4, 4], replicated, may hold values 0 or 1
Outputs:
- attended: bfloat16 [8192, 3072], P(('seq', 'head'))
- grad_query: bfloat16 [8192, 3072], P(('seq', 'head'))
- grad_keys: bfloat16 [8192, 3072], P(('seq', 'head'))
- grad_values: bfloat16 [8192, 3072], P(('seq', 'head'))
The draws below stay inside these ranges and needn't reach their ends.
All inputs are finite; a program needn't handle non-finite values.
Results may differ from the reference program's by a relative error of at most 0.024.
Values may be sent and summed in bfloat16 or wider, within the bound.
A program may use at most 64 MiB of HBM per device.

```python
import math
import jax
import jax.numpy as jnp
from jax import lax

HD = 128
HEADS = 24
BLOCK = 128
GROUP = 4
F_TOK = 512
NB = 4
LEVELS = 4
TOKENS = 8192


def draw_query_rows(key, part):
    row_count = TOKENS
    col_count = HEADS * HD
    drawn = jnp.clip(jax.random.normal(jax.random.fold_in(key, 1), (row_count, col_count), jnp.float32), -5.0, 5.0)
    return drawn.astype(jnp.bfloat16)


def draw_key_rows(key, part):
    row_count = TOKENS
    col_count = HEADS * HD
    drawn = jnp.clip(jax.random.normal(jax.random.fold_in(key, 2), (row_count, col_count), jnp.float32), -5.0, 5.0)
    return drawn.astype(jnp.bfloat16)


def with_ends(result, rng, low, top_value):
    spot = [jax.random.randint(jax.random.fold_in(rng, axis), (), 0, length) for axis, length in enumerate(result.shape)]
    main_axis = result.shape.index(max(result.shape))
    next_to = spot[:main_axis] + [(spot[main_axis] + 1) % result.shape[main_axis]] + spot[main_axis + 1:]
    return result.at[tuple(spot)].set(low).at[tuple(next_to)].set(top_value)


def levels(stream_key, extent, cuts, least, high):
    loudness = 1.0
    for axis_at, parts in cuts:
        heights = jax.random.uniform(jax.random.fold_in(jax.random.fold_in(stream_key, 6), axis_at), (parts,), jnp.float32, least / len(cuts), high / len(cuts))
        loudness = loudness * jnp.repeat(jnp.exp(heights), extent[axis_at] // parts).reshape((-1,) + (1,) * (len(extent) - 1 - axis_at))
    return loudness


def bell_draw(rng, shape, spread, limit, pieces=(), dtype=jnp.bfloat16):
    gain = levels(rng, shape, pieces, -0.22, 0.18) if pieces else 1.0
    values = jax.random.normal(rng, shape, jnp.float32) * spread * gain
    return jnp.minimum(jnp.maximum(values, -limit), limit).astype(dtype)


def setup_inputs(seed: int = 0) -> dict:
    keys = jax.random.split(jax.random.key(seed), 6)
    query_rows = draw_query_rows(jax.random.fold_in(keys[5], 71), 0)
    key_rows = draw_key_rows(jax.random.fold_in(keys[5], 71), 0)
    value_rows = bell_draw(keys[2], (TOKENS, HEADS * HD), 1.0, 6.0, ((0, 512),))
    out_grad = bell_draw(keys[3], (TOKENS, HEADS * HD), 1.0, 6.0, ((0, 512),))
    block_mask = with_ends((jax.random.randint(keys[4], (LEVELS, NB, NB), 0, 2) < 1).astype(jnp.int32), jax.random.fold_in(keys[4], 1), 0, 1)
    return {"query_rows": query_rows, "key_rows": key_rows, "value_rows": value_rows, "out_grad": out_grad, "block_mask": block_mask}


def widen_mask(bits):
    blocks = bits.shape[0]
    grid = jnp.broadcast_to((bits > 0)[:, None, :, None], (blocks, BLOCK, blocks, BLOCK))
    return grid.reshape(blocks * BLOCK, blocks * BLOCK)

def reference(query_rows, key_rows, value_rows, out_grad, block_mask):
    token_count, width = query_rows.shape
    frame_count = token_count // F_TOK
    head_count = width // HD
    block_rows = F_TOK // GROUP
    score_scale = 1.0 / math.sqrt(HD)

    def framed(rows):
        return rows.reshape(frame_count, F_TOK, head_count, HD)
    query_f, key_f, value_f, grad_f = (framed(query_rows), framed(key_rows), framed(value_rows), framed(out_grad))
    level_masks = [widen_mask(block_mask[level_index]) for level_index in range(LEVELS)]
    offsets = [0]
    for level_index in range(LEVELS):
        for orient in (1, -1):
            offsets.append(-orient * (1 << level_index))

    def one_frame(frame_index, carry):
        out_acc, dq_acc, dk_acc, dv_acc = carry
        allowed_list = [jnp.ones((F_TOK, F_TOK), bool)]
        spot = 1
        for level_index in range(LEVELS):
            for orient in (1, -1):
                partner = frame_index + offsets[spot]
                inside = (partner >= 0) & (partner < frame_count)
                allowed_list.append(level_masks[level_index] & inside)
                spot += 1
        allowed = jnp.concatenate(allowed_list, axis=1)
        places = [jnp.clip(frame_index + shift_by, 0, frame_count - 1).astype(jnp.int32) for shift_by in offsets]
        keys_all = jnp.concatenate([lax.dynamic_index_in_dim(key_f, place, 0, keepdims=False) for place in places], axis=0).astype(jnp.float32)
        values_all = jnp.concatenate([lax.dynamic_index_in_dim(value_f, place, 0, keepdims=False) for place in places], axis=0).astype(jnp.float32)
        query_now = lax.dynamic_index_in_dim(query_f, frame_index, 0, keepdims=False).astype(jnp.float32)
        grad_now = lax.dynamic_index_in_dim(grad_f, frame_index, 0, keepdims=False).astype(jnp.float32)
        scores = jnp.einsum('qhd,khd->hqk', query_now, keys_all) * score_scale
        scores = jnp.where(allowed[None], scores, -jnp.inf)
        peak = lax.optimization_barrier(jnp.max(scores, axis=2, keepdims=True))
        logsum = peak + jnp.log(lax.optimization_barrier(jnp.sum(jnp.exp(scores - peak), axis=2, keepdims=True)))
        probability = jnp.exp(scores - logsum)
        weights = probability.astype(jnp.bfloat16)
        weights32 = weights.astype(jnp.float32)
        attended = jnp.einsum('hqk,khd->qhd', weights32, values_all).astype(jnp.bfloat16)
        grad_weights = jnp.einsum('qhd,khd->hqk', grad_now, values_all)
        delta = jnp.transpose(lax.optimization_barrier(jnp.sum(grad_now * attended.astype(jnp.float32), axis=2)))[:, :, None]
        grad_scores = (probability * (grad_weights - delta) * score_scale).astype(jnp.bfloat16)
        scores32 = grad_scores.astype(jnp.float32)
        grad_q = jnp.einsum('hqk,khd->qhd', scores32, keys_all).astype(jnp.bfloat16)
        key_count = scores32.shape[2]
        key_part = jnp.einsum('hgqk,gqhd->gkhd', scores32.reshape(head_count, GROUP, block_rows, key_count), query_now.reshape(GROUP, block_rows, head_count, HD))
        value_part = jnp.einsum('hgqk,gqhd->gkhd', weights32.reshape(head_count, GROUP, block_rows, key_count), grad_now.reshape(GROUP, block_rows, head_count, HD))
        key_part = lax.optimization_barrier(key_part.astype(jnp.bfloat16)).astype(jnp.float32).sum(axis=0)
        value_part = lax.optimization_barrier(value_part.astype(jnp.bfloat16)).astype(jnp.float32).sum(axis=0)
        key_part = key_part.reshape(len(offsets), F_TOK, head_count, HD)
        value_part = value_part.reshape(len(offsets), F_TOK, head_count, HD)
        for spot_index, place in enumerate(places):
            dk_acc = dk_acc.at[place].add(key_part[spot_index])
            dv_acc = dv_acc.at[place].add(value_part[spot_index])
        out_acc = lax.dynamic_update_index_in_dim(out_acc, attended, frame_index, 0)
        dq_acc = lax.dynamic_update_index_in_dim(dq_acc, grad_q, frame_index, 0)
        return (out_acc, dq_acc, dk_acc, dv_acc)
    shape = (frame_count, F_TOK, head_count, HD)
    start = (jnp.zeros(shape, jnp.bfloat16), jnp.zeros(shape, jnp.bfloat16), jnp.zeros(shape, jnp.float32), jnp.zeros(shape, jnp.float32))
    out_acc, dq_acc, dk_acc, dv_acc = lax.fori_loop(0, frame_count, one_frame, start)
    return (out_acc.reshape(token_count, width), dq_acc.reshape(token_count, width), dk_acc.astype(jnp.bfloat16).reshape(token_count, width), dv_acc.astype(jnp.bfloat16).reshape(token_count, width))
```

```python
import math

import jax
import jax.numpy as jnp
from jax import lax
from jax.experimental import pallas as pl
from jax.experimental.pallas import tpu as pltpu
from jax.sharding import PartitionSpec as P

HD = 128
HEADS = 24
FT = 512
FRAMES = 16
SUB = 16
OWNERS = 32
PLANES = 8
PER_PLANE = 3
UNITS = 8
SCALE = 1.0 / math.sqrt(HD)
EXP2 = SCALE * math.log2(math.e)
BF = jnp.bfloat16
F32 = jnp.float32


def place(head, frame):
    plane = head // PER_PLANE
    pair = (head % PER_PLANE + plane) % 4
    col = frame % 4
    seq = ((frame // 4) * 8 + 2 * pair + col % 2) * 2 + col // 2
    return seq, plane


def shift_of(rel):
    return (1 - 2 * (rel % 2)) * lax.shift_left(jnp.int32(1), rel // 2)


def inside(frame):
    return (frame >= 0) & (frame < FRAMES)


def sent_to(frame, rel):
    there = jnp.where(rel == 6, (frame + 8) % FRAMES, frame + shift_of(rel))
    return there, inside(there)


def came_from(frame, rel):
    there = jnp.where(rel == 6, (frame + 8) % FRAMES, frame - shift_of(rel))
    return there, inside(there)


def attention_kernel(
    q_in, k_in, v_in, g_in, mask,
    o_out, dq_out, dk_out, dv_out,
    rows, kv, qg, scores, gradw, weights, scores_b, parts, back, outs,
    peak, acc, dq_acc, rowl, rowd, qt, gt, bias,
    in_sem, s1, r1, s2, r2, s3, r3, s4, r4,
):
    seq = lax.axis_index("seq")
    plane = lax.axis_index("head")
    src_frame = seq // 4
    src_spot = (seq % 4) * 8 + plane
    a = seq // 16
    y = (seq // 2) % 8
    col = (seq % 2) * 2 + y % 2
    frame = 4 * a + col
    within = (y // 2 + 8 - plane) % 4
    busy = within < PER_PLANE
    head = plane * PER_PLANE + within
    own_hit = busy & (frame == src_frame)

    def is_me(target):
        return (target[0] == seq) & (target[1] == plane)

    def owner(spot):
        return frame * 4 + spot // 8, spot % 8

    fetch = [
        pltpu.make_async_copy(ref, rows.at[n], in_sem.at[n])
        for n, ref in enumerate((k_in, v_in, q_in, g_in))
    ]
    for copy in fetch:
        copy.start()

    barrier = pltpu.get_barrier_semaphore()

    def greet(target):
        @pl.when(jnp.logical_not(is_me(target)))
        def _():
            pl.semaphore_signal(
                barrier, inc=1, device_id=target, device_id_type=pl.DeviceIdType.MESH
            )

    def greet_head(n, carry):
        greet(place(n, src_frame))
        return carry

    lax.fori_loop(0, HEADS, greet_head, 0)

    @pl.when(busy)
    def _():
        def greet_owner(n, carry):
            greet(owner(n))
            return carry

        lax.fori_loop(0, OWNERS, greet_owner, 0)

        def greet_partner(rel, carry):
            there, ok = sent_to(frame, rel)

            @pl.when(ok)
            def _():
                greet(place(head, there))

            return carry

        lax.fori_loop(0, UNITS - 1, greet_partner, 0)

    partners = jnp.int32(0)
    for rel in range(UNITS - 1):
        partners = partners + came_from(frame, jnp.int32(rel))[1].astype(jnp.int32)
    hit = own_hit.astype(jnp.int32)
    expected = HEADS - hit + busy.astype(jnp.int32) * (OWNERS - hit + partners)
    for copy in fetch:
        copy.wait()
    pl.semaphore_wait(barrier, expected)

    def scatter(stage, dst):
        def piece(n):
            k = n // PER_PLANE
            off = (4 + ((k + 1) // 2) * (2 * (k % 2) - 1) + 8) % 8
            to_head = ((plane + off) % PLANES) * PER_PLANE + n % PER_PLANE
            target = place(to_head, src_frame)
            src = rows.at[
                pl.ds(2 * stage, 2), :, pl.ds(pl.multiple_of(to_head * HD, HD), HD)
            ]
            to = dst.at[:, pl.ds(pl.multiple_of(src_spot * SUB, SUB), SUB), :]
            return target, src, to

        def remote(target, src, to):
            return pltpu.make_async_remote_copy(
                src_ref=src, dst_ref=to, send_sem=s1.at[stage], recv_sem=r1.at[stage],
                device_id=target, device_id_type=pl.DeviceIdType.MESH,
            )

        def send(n, carry):
            target, src, to = piece(n)
            mine = is_me(target)

            @pl.when(mine)
            def _():
                pltpu.make_async_copy(src, to, r1.at[stage]).start()

            @pl.when(jnp.logical_not(mine))
            def _():
                remote(target, src, to).start()

            return carry

        def sent(n, carry):
            target, src, to = piece(n)

            @pl.when(jnp.logical_not(is_me(target)))
            def _():
                remote(target, src, to).wait_send()

            return carry

        return send, sent

    send_kv, sent_kv = scatter(0, kv.at[0])
    send_qg, sent_qg = scatter(1, qg)
    lax.fori_loop(0, HEADS, send_kv, 0)
    lax.fori_loop(0, HEADS, send_qg, 0)

    def kv_copy(rel):
        there, ok = sent_to(frame, rel)
        copy = pltpu.make_async_remote_copy(
            src_ref=kv.at[0], dst_ref=kv.at[rel + 1], send_sem=s2.at[rel], recv_sem=r2.at[rel],
            device_id=place(head, there), device_id_type=pl.DeviceIdType.MESH,
        )
        return copy, ok

    def grad_copy(rel):
        there, ok = came_from(frame, rel)
        copy = pltpu.make_async_remote_copy(
            src_ref=parts.at[rel + 1], dst_ref=back.at[rel], send_sem=s3.at[rel],
            recv_sem=r3.at[rel],
            device_id=place(head, there), device_id_type=pl.DeviceIdType.MESH,
        )
        return copy, ok

    def result_copy(array, spot):
        target = owner(spot)
        src = outs.at[array, pl.ds(pl.multiple_of(spot * SUB, SUB), SUB), :]
        dst = (o_out, dq_out, dk_out, dv_out)[array].at[
            :, pl.ds(pl.multiple_of(head * HD, HD), HD)
        ]
        remote = pltpu.make_async_remote_copy(
            src_ref=src, dst_ref=dst, send_sem=s4.at[array], recv_sem=r4.at[array],
            device_id=target, device_id_type=pl.DeviceIdType.MESH,
        )
        return is_me(target), remote, pltpu.make_async_copy(src, dst, r4.at[array])

    def give_result(array):
        def send(spot, carry):
            mine, remote, local = result_copy(array, spot)

            @pl.when(mine)
            def _():
                local.start()

            @pl.when(jnp.logical_not(mine))
            def _():
                remote.start()

            return carry

        lax.fori_loop(0, OWNERS, send, 0)

    @pl.when(busy)
    def _():
        pltpu.make_async_copy(kv.at[0], kv.at[0], r1.at[0]).wait()

        def send_partner(rel, carry):
            copy, ok = kv_copy(rel)

            @pl.when(ok)
            def _():
                copy.start()

            return carry

        lax.fori_loop(0, UNITS - 1, send_partner, 0)

        lane_block = lax.broadcasted_iota(jnp.int32, (8, FT), 1) // 128
        bias[16] = jnp.zeros((8, FT), F32)

        def bias_row(n, carry):
            row = jnp.zeros((8, FT), F32)
            for kb in range(4):
                seen = mask[n // 4, n % 4, kb] > 0
                row = jnp.where(
                    (lane_block == kb) & jnp.logical_not(seen), jnp.float32(-jnp.inf), row
                )
            bias[n] = row
            return carry

        lax.fori_loop(0, 16, bias_row, 0)
        peak[...] = jnp.full((FT, HD), -jnp.inf, F32)
        acc[...] = jnp.zeros((FT, HD), F32)
        dq_acc[...] = jnp.zeros((FT, HD), F32)
        rowl[...] = jnp.zeros((FT, HD), F32)

        pltpu.make_async_copy(qg, qg, r1.at[1]).wait()
        qt[...] = qg[0].T

        def has_unit(u):
            return (u == 0) | came_from(frame, u - 1 + (u == 0).astype(jnp.int32))[1]

        def first_pass(u, carry):
            @pl.when(has_unit(u))
            def _():
                @pl.when(u > 0)
                def _():
                    pltpu.make_async_copy(kv.at[u], kv.at[u], r2.at[u - 1]).wait()

                keys = kv[u, 0]
                values = kv[u, 1]
                for qb in range(4):
                    band = pl.ds(qb * 128, 128)
                    which = jnp.where(u == 0, 16, ((u + 1) // 2 - 1) * 4 + qb)
                    s = lax.dot_general(
                        qg[0, band], keys, (((1,), (1,)), ((), ())), preferred_element_type=F32
                    )
                    s = s + bias[which, 0:1, :]
                    scores[u, band] = s
                    top = jnp.maximum(
                        jnp.maximum(s[:, 0:128], s[:, 128:256]),
                        jnp.maximum(s[:, 256:384], s[:, 384:512]),
                    )
                    peak[band] = jnp.maximum(peak[band], top)
                    gradw[u, band] = lax.dot_general(
                        qg[1, band], values, (((1,), (1,)), ((), ())), preferred_element_type=F32
                    )

            return carry

        lax.fori_loop(0, UNITS, first_pass, 0)
        top = jnp.max(peak[...], axis=1, keepdims=True) * EXP2
        peak[...] = jnp.broadcast_to(top, (FT, HD))

        def second_pass(u, carry):
            @pl.when(has_unit(u))
            def _():
                for qb in range(4):
                    band = pl.ds(qb * 128, 128)
                    e = jnp.exp2(scores[u, band] * EXP2 - peak[band, 0:1])
                    rowl[band] += (e[:, 0:128] + e[:, 128:256]) + (e[:, 256:384] + e[:, 384:512])
                    weights[u, band] = e.astype(BF)
                acc[...] += jnp.dot(weights[u], kv[u, 1], preferred_element_type=F32)

            return carry

        lax.fori_loop(0, UNITS, second_pass, 0)
        inv = 1.0 / jnp.sum(rowl[...], axis=1, keepdims=True)
        attended = (acc[...] * inv).astype(BF)
        outs[0] = attended
        give_result(0)
        grads = qg[1].astype(F32)
        delta = jnp.sum(grads * attended.astype(F32), axis=1, keepdims=True)
        gt[...] = (grads * inv).astype(BF).T
        inv = inv * SCALE
        rowl[...] = jnp.broadcast_to(inv, (FT, HD))
        rowd[...] = jnp.broadcast_to(inv * delta, (FT, HD))

        def third_pass(n, carry):
            u = UNITS - 1 - n

            @pl.when(has_unit(u))
            def _():
                for qb in range(4):
                    band = pl.ds(qb * 128, 128)
                    ds = weights[u, band].astype(F32) * (
                        gradw[u, band] * rowl[band, 0:1] - rowd[band, 0:1]
                    )
                    scores_b[u, band] = ds.astype(BF)
                ds = scores_b[u]
                parts[u, 0] = jnp.dot(qt[...], ds, preferred_element_type=F32).astype(BF)
                parts[u, 1] = jnp.dot(gt[...], weights[u], preferred_element_type=F32).astype(BF)

                @pl.when(u > 0)
                def _():
                    grad_copy(u - 1)[0].start()

                dq_acc[...] += jnp.dot(ds, kv[u, 0], preferred_element_type=F32)

            return carry

        lax.fori_loop(0, UNITS, third_pass, 0)
        outs[1] = dq_acc[...].astype(BF)
        give_result(1)

        sums = scores.at[0, pl.ds(0, 256)]
        sums[0:128] = parts[0, 0].astype(F32)
        sums[128:256] = parts[0, 1].astype(F32)

        def add_back(rel, carry):
            @pl.when(sent_to(frame, rel)[1])
            def _():
                pltpu.make_async_copy(back.at[rel], back.at[rel], r3.at[rel]).wait()
                sums[0:128] += back[rel, 0].astype(F32)
                sums[128:256] += back[rel, 1].astype(F32)

            return carry

        lax.fori_loop(0, UNITS - 1, add_back, 0)
        outs[2] = sums[0:128].T.astype(BF)
        give_result(2)
        outs[3] = sums[128:256].T.astype(BF)
        give_result(3)

        def partner_sent(rel, carry):
            copy, ok = kv_copy(rel)

            @pl.when(ok)
            def _():
                copy.wait_send()

            copy, ok = grad_copy(rel)

            @pl.when(ok)
            def _():
                copy.wait_send()

            return carry

        lax.fori_loop(0, UNITS - 1, partner_sent, 0)
        for array in range(4):

            def result_sent(spot, carry, array=array):
                mine, remote, _ = result_copy(array, spot)

                @pl.when(jnp.logical_not(mine))
                def _():
                    remote.wait_send()

                return carry

            lax.fori_loop(0, OWNERS, result_sent, 0)

    lax.fori_loop(0, HEADS, sent_kv, 0)
    lax.fori_loop(0, HEADS, sent_qg, 0)
    for n, ref in enumerate((o_out, dq_out, dk_out, dv_out)):
        pltpu.make_async_copy(ref, ref, r4.at[n]).wait()


def per_device(query_rows, key_rows, value_rows, out_grad, block_mask):
    anywhere = pl.BlockSpec(memory_space=pl.ANY)
    result = jax.ShapeDtypeStruct(query_rows.shape, BF)
    dma = pltpu.SemaphoreType.DMA
    return pl.pallas_call(
        attention_kernel,
        out_shape=(result,) * 4,
        in_specs=[anywhere] * 4 + [pl.BlockSpec(memory_space=pltpu.SMEM)],
        out_specs=(anywhere,) * 4,
        scratch_shapes=[
            pltpu.VMEM((4, SUB, HEADS * HD), BF),
            pltpu.VMEM((UNITS, 2, FT, HD), BF),
            pltpu.VMEM((2, FT, HD), BF),
            pltpu.VMEM((UNITS, FT, FT), F32),
            pltpu.VMEM((UNITS, FT, FT), F32),
            pltpu.VMEM((UNITS, FT, FT), BF),
            pltpu.VMEM((UNITS, FT, FT), BF),
            pltpu.VMEM((UNITS, 2, HD, FT), BF),
            pltpu.VMEM((UNITS - 1, 2, HD, FT), BF),
            pltpu.VMEM((4, FT, HD), BF),
            pltpu.VMEM((FT, HD), F32),
            pltpu.VMEM((FT, HD), F32),
            pltpu.VMEM((FT, HD), F32),
            pltpu.VMEM((FT, HD), F32),
            pltpu.VMEM((FT, HD), F32),
            pltpu.VMEM((HD, FT), BF),
            pltpu.VMEM((HD, FT), BF),
            pltpu.VMEM((17, 8, FT), F32),
            dma((4,)),
            dma((2,)),
            dma((2,)),
            dma((UNITS - 1,)),
            dma((UNITS - 1,)),
            dma((UNITS - 1,)),
            dma((UNITS - 1,)),
            dma((4,)),
            dma((4,)),
        ],
        compiler_params=pltpu.CompilerParams(
            collective_id=0, has_side_effects=True, vmem_limit_bytes=48 * 1024 * 1024
        ),
    )(query_rows, key_rows, value_rows, out_grad, block_mask)


def solution(mesh):
    tokens = P(("seq", "head"), None)
    return jax.shard_map(
        per_device,
        mesh=mesh,
        in_specs=(tokens,) * 4 + (P(),),
        out_specs=(tokens,) * 4,
        check_vma=False,
    )
```

```python
import math

import jax
import jax.numpy as jnp
from jax import lax
from jax.experimental import pallas as pl
from jax.experimental.pallas import tpu as pltpu
from jax.sharding import PartitionSpec as P

HD = 128
HEADS = 24
FT = 512
FRAMES = 16
SUB = 16
OWNERS = 32
PLANES = 8
PER_PLANE = 3
UNITS = 8
SCALE = 1.0 / math.sqrt(HD)
EXP2 = SCALE * math.log2(math.e)
BF = jnp.bfloat16
F32 = jnp.float32
VMEM_MB = 60


def seat(pair, frame):
    return (frame >> 2) * 16 + pair * 4 + (frame & 1) * 2 + ((frame >> 1) & 1)


def shift_of(rel):
    return (1 - 2 * (rel & 1)) * lax.shift_left(jnp.int32(1), rel >> 1)


def inside(frame):
    return (frame >= 0) & (frame < FRAMES)


def sent_to(frame, rel):
    there = jnp.where(rel == 6, (frame + 8) & 15, frame + shift_of(rel))
    return there, inside(there)


def came_from(frame, rel):
    there = jnp.where(rel == 6, (frame + 8) & 15, frame - shift_of(rel))
    return there, inside(there)


def attention_kernel(
    q_in, k_in, v_in, g_in, mask,
    o_out, dq_out, dk_out, dv_out,
    rows, kv, qg, scores, gradw, weights, scores_b, parts, back, outs,
    peak, acc, dq_acc, rowl, rowd, qt, gt, bias,
    in_sem, s1, r1, s2, r2, s3, r3, s4, r4,
):
    seq = lax.axis_index("seq")
    plane = lax.axis_index("head")
    src_frame = seq >> 2
    src_spot = (seq & 3) * 8 + plane
    frame = (seq >> 4) * 4 + (seq & 1) * 2 + ((seq >> 1) & 1)
    pair = (seq >> 2) & 3
    within = (pair - plane) & 3
    busy = within < PER_PLANE
    head = plane * PER_PLANE + within
    own_hit = busy & (frame == src_frame)
    my_head = jnp.where(own_hit, head, -1)
    my_spot = jnp.where(own_hit, src_spot, -1)
    seat0 = seat(0, src_frame)

    fetch = [
        pltpu.make_async_copy(ref, rows.at[n], in_sem.at[n])
        for n, ref in enumerate((k_in, v_in, q_in, g_in))
    ]
    for copy in fetch:
        copy.start()

    barrier = pltpu.get_barrier_semaphore()

    def greet(target):
        pl.semaphore_signal(
            barrier, inc=1, device_id=target, device_id_type=pl.DeviceIdType.MESH
        )

    @pl.when(busy)
    def _():
        def greet_owners(z, carry):
            for r in range(4):
                greet((frame * 4 + r, z))

            return carry

        lax.fori_loop(0, PLANES, greet_owners, 0)

        def greet_partner(rel, carry):
            there, ok = sent_to(frame, rel)

            @pl.when(ok)
            def _():
                greet((seat(pair, there), plane))

            return carry

        lax.fori_loop(0, UNITS - 1, greet_partner, 0)

    partners = jnp.int32(0)
    for rel in range(UNITS - 1):
        partners = partners + came_from(frame, jnp.int32(rel))[1].astype(jnp.int32)
    expected = HEADS + busy.astype(jnp.int32) * partners
    for copy in fetch:
        copy.wait()
    pl.semaphore_wait(barrier, expected)

    def scatter(stage, dst):
        to = dst.at[:, pl.ds(pl.multiple_of(src_spot * SUB, SUB), SUB), :]

        def send(k, carry):
            off = 4 + ((k + 1) >> 1) * (2 * (k & 1) - 1)
            z = (plane + off) & 7
            for c in range(PER_PLANE):
                to_head = z * PER_PLANE + c
                src = rows.at[
                    pl.ds(2 * stage, 2), :, pl.ds(pl.multiple_of(to_head * HD, HD), HD)
                ]
                mine = to_head == my_head

                @pl.when(mine)
                def _(src=src):
                    pltpu.make_async_copy(src, to, r1.at[stage]).start()

                @pl.when(jnp.logical_not(mine))
                def _(src=src, c=c):
                    pltpu.make_async_remote_copy(
                        src_ref=src, dst_ref=to, send_sem=s1.at[stage], recv_sem=r1.at[stage],
                        device_id=(seat0 + ((c + z) & 3) * 4, z),
                        device_id_type=pl.DeviceIdType.MESH,
                    ).start()

            return carry

        lax.fori_loop(0, PLANES, send, 0)

    def wait_for(ref, sem):
        pltpu.make_async_copy(ref, ref, sem).wait()

    scatter(0, kv.at[0])
    scatter(1, qg)

    def kv_copy(rel):
        there, ok = sent_to(frame, rel)
        copy = pltpu.make_async_remote_copy(
            src_ref=kv.at[0], dst_ref=kv.at[rel + 1], send_sem=s2.at[rel], recv_sem=r2.at[rel],
            device_id=(seat(pair, there), plane), device_id_type=pl.DeviceIdType.MESH,
        )
        return copy, ok

    def grad_copy(rel):
        there, ok = came_from(frame, rel)
        copy = pltpu.make_async_remote_copy(
            src_ref=parts.at[rel + 1], dst_ref=back.at[rel], send_sem=s3.at[rel],
            recv_sem=r3.at[rel],
            device_id=(seat(pair, there), plane), device_id_type=pl.DeviceIdType.MESH,
        )
        return copy, ok

    def give_result(array):
        dst = (o_out, dq_out, dk_out, dv_out)[array].at[
            :, pl.ds(pl.multiple_of(head * HD, HD), HD)
        ]

        def send(z, carry):
            for r in range(4):
                spot = r * 8 + z
                src = outs.at[array, pl.ds(pl.multiple_of(spot * SUB, SUB), SUB), :]
                mine = spot == my_spot

                @pl.when(mine)
                def _(src=src):
                    pltpu.make_async_copy(src, dst, r4.at[array]).start()

                @pl.when(jnp.logical_not(mine))
                def _(src=src, r=r):
                    pltpu.make_async_remote_copy(
                        src_ref=src, dst_ref=dst, send_sem=s4.at[array], recv_sem=r4.at[array],
                        device_id=(frame * 4 + r, z), device_id_type=pl.DeviceIdType.MESH,
                    ).start()

            return carry

        lax.fori_loop(0, PLANES, send, 0)

    @pl.when(busy)
    def _():
        pltpu.make_async_copy(kv.at[0], kv.at[0], r1.at[0]).wait()

        def send_partner(rel, carry):
            copy, ok = kv_copy(rel)

            @pl.when(ok)
            def _():
                copy.start()

            return carry

        lax.fori_loop(0, UNITS - 1, send_partner, 0)

        lane_block = lax.broadcasted_iota(jnp.int32, (8, FT), 1) // 128
        bias[16] = jnp.zeros((8, FT), F32)

        def bias_row(n, carry):
            row = jnp.zeros((8, FT), F32)
            for kb in range(4):
                seen = mask[n // 4, n % 4, kb] > 0
                row = jnp.where(
                    (lane_block == kb) & jnp.logical_not(seen), jnp.float32(-jnp.inf), row
                )
            bias[n] = row
            return carry

        lax.fori_loop(0, 16, bias_row, 0)
        peak[...] = jnp.full((FT, HD), -jnp.inf, F32)
        acc[...] = jnp.zeros((FT, HD), F32)
        dq_acc[...] = jnp.zeros((FT, HD), F32)
        rowl[...] = jnp.zeros((FT, HD), F32)

        pltpu.make_async_copy(qg, qg, r1.at[1]).wait()
        qt[...] = qg[0].T

        def has_unit(u):
            return (u == 0) | came_from(frame, u - 1 + (u == 0).astype(jnp.int32))[1]

        def first_pass(u, carry):
            @pl.when(has_unit(u))
            def _():
                @pl.when(u > 0)
                def _():
                    pltpu.make_async_copy(kv.at[u], kv.at[u], r2.at[u - 1]).wait()

                keys = kv[u, 0]
                values = kv[u, 1]
                for qb in range(4):
                    band = pl.ds(qb * 128, 128)
                    which = jnp.where(u == 0, 16, ((u + 1) // 2 - 1) * 4 + qb)
                    s = lax.dot_general(
                        qg[0, band], keys, (((1,), (1,)), ((), ())), preferred_element_type=F32
                    )
                    s = s + bias[which, 0:1, :]
                    scores[u, band] = s
                    top = jnp.maximum(
                        jnp.maximum(s[:, 0:128], s[:, 128:256]),
                        jnp.maximum(s[:, 256:384], s[:, 384:512]),
                    )
                    peak[band] = jnp.maximum(peak[band], top)
                    gradw[u, band] = lax.dot_general(
                        qg[1, band], values, (((1,), (1,)), ((), ())), preferred_element_type=F32
                    )

            return carry

        lax.fori_loop(0, UNITS, first_pass, 0)
        top = jnp.max(peak[...], axis=1, keepdims=True) * EXP2
        peak[...] = jnp.broadcast_to(top, (FT, HD))

        def second_pass(u, carry):
            @pl.when(has_unit(u))
            def _():
                for qb in range(4):
                    band = pl.ds(qb * 128, 128)
                    e = jnp.exp2(scores[u, band] * EXP2 - peak[band, 0:1])
                    rowl[band] += (e[:, 0:128] + e[:, 128:256]) + (e[:, 256:384] + e[:, 384:512])
                    weights[u, band] = e.astype(BF)
                acc[...] += jnp.dot(weights[u], kv[u, 1], preferred_element_type=F32)

            return carry

        lax.fori_loop(0, UNITS, second_pass, 0)
        inv = 1.0 / jnp.sum(rowl[...], axis=1, keepdims=True)
        attended = (acc[...] * inv).astype(BF)
        outs[0] = attended
        give_result(0)
        grads = qg[1].astype(F32)
        delta = jnp.sum(grads * attended.astype(F32), axis=1, keepdims=True)
        gt[...] = (grads * inv).astype(BF).T
        inv = inv * SCALE
        rowl[...] = jnp.broadcast_to(inv, (FT, HD))
        rowd[...] = jnp.broadcast_to(inv * delta, (FT, HD))

        def third_pass(n, carry):
            u = UNITS - 1 - n

            @pl.when(has_unit(u))
            def _():
                for qb in range(4):
                    band = pl.ds(qb * 128, 128)
                    ds = weights[u, band].astype(F32) * (
                        gradw[u, band] * rowl[band, 0:1] - rowd[band, 0:1]
                    )
                    scores_b[u, band] = ds.astype(BF)
                ds = scores_b[u]
                parts[u, 0] = jnp.dot(qt[...], ds, preferred_element_type=F32).astype(BF)
                parts[u, 1] = jnp.dot(gt[...], weights[u], preferred_element_type=F32).astype(BF)

                @pl.when(u > 0)
                def _():
                    grad_copy(u - 1)[0].start()

                dq_acc[...] += jnp.dot(ds, kv[u, 0], preferred_element_type=F32)

            return carry

        lax.fori_loop(0, UNITS, third_pass, 0)
        outs[1] = dq_acc[...].astype(BF)
        give_result(1)

        sums = scores.at[0, pl.ds(0, 256)]
        sums[0:128] = parts[0, 0].astype(F32)
        sums[128:256] = parts[0, 1].astype(F32)

        def add_back(rel, carry):
            @pl.when(sent_to(frame, rel)[1])
            def _():
                pltpu.make_async_copy(back.at[rel], back.at[rel], r3.at[rel]).wait()
                sums[0:128] += back[rel, 0].astype(F32)
                sums[128:256] += back[rel, 1].astype(F32)

            return carry

        lax.fori_loop(0, UNITS - 1, add_back, 0)
        outs[2] = sums[0:128].T.astype(BF)
        give_result(2)
        outs[3] = sums[128:256].T.astype(BF)
        give_result(3)

        def partner_sent(rel, carry):
            copy, ok = kv_copy(rel)

            @pl.when(ok)
            def _():
                copy.wait_send()

            copy, ok = grad_copy(rel)

            @pl.when(ok)
            def _():
                copy.wait_send()

            return carry

        lax.fori_loop(0, UNITS - 1, partner_sent, 0)
        for array in range(4):

            @pl.when(own_hit)
            def _(array=array):
                wait_for(outs.at[array, pl.ds(0, FT - SUB)], s4.at[array])

            @pl.when(jnp.logical_not(own_hit))
            def _(array=array):
                wait_for(outs.at[array], s4.at[array])

    for stage in range(2):
        sent = rows.at[pl.ds(2 * stage, 2)]

        @pl.when(own_hit)
        def _(sent=sent, stage=stage):
            wait_for(sent.at[:, :, pl.ds(0, (HEADS - 1) * HD)], s1.at[stage])

        @pl.when(jnp.logical_not(own_hit))
        def _(sent=sent, stage=stage):
            wait_for(sent, s1.at[stage])

    for n, ref in enumerate((o_out, dq_out, dk_out, dv_out)):
        pltpu.make_async_copy(ref, ref, r4.at[n]).wait()


def per_device(query_rows, key_rows, value_rows, out_grad, block_mask):
    anywhere = pl.BlockSpec(memory_space=pl.ANY)
    result = jax.ShapeDtypeStruct(query_rows.shape, BF)
    dma = pltpu.SemaphoreType.DMA
    return pl.pallas_call(
        attention_kernel,
        out_shape=(result,) * 4,
        in_specs=[anywhere] * 4 + [pl.BlockSpec(memory_space=pltpu.SMEM)],
        out_specs=(anywhere,) * 4,
        scratch_shapes=[
            pltpu.VMEM((4, SUB, HEADS * HD), BF),
            pltpu.VMEM((UNITS, 2, FT, HD), BF),
            pltpu.VMEM((2, FT, HD), BF),
            pltpu.VMEM((UNITS, FT, FT), F32),
            pltpu.VMEM((UNITS, FT, FT), F32),
            pltpu.VMEM((UNITS, FT, FT), BF),
            pltpu.VMEM((UNITS, FT, FT), BF),
            pltpu.VMEM((UNITS, 2, HD, FT), BF),
            pltpu.VMEM((UNITS - 1, 2, HD, FT), BF),
            pltpu.VMEM((4, FT, HD), BF),
            pltpu.VMEM((FT, HD), F32),
            pltpu.VMEM((FT, HD), F32),
            pltpu.VMEM((FT, HD), F32),
            pltpu.VMEM((FT, HD), F32),
            pltpu.VMEM((FT, HD), F32),
            pltpu.VMEM((HD, FT), BF),
            pltpu.VMEM((HD, FT), BF),
            pltpu.VMEM((17, 8, FT), F32),
            dma((4,)),
            dma((2,)),
            dma((2,)),
            dma((UNITS - 1,)),
            dma((UNITS - 1,)),
            dma((UNITS - 1,)),
            dma((UNITS - 1,)),
            dma((4,)),
            dma((4,)),
        ],
        compiler_params=pltpu.CompilerParams(
            collective_id=0, has_side_effects=True, vmem_limit_bytes=VMEM_MB * 1024 * 1024
        ),
    )(query_rows, key_rows, value_rows, out_grad, block_mask)


def solution(mesh):
    tokens = P(("seq", "head"), None)
    return jax.shard_map(
        per_device,
        mesh=mesh,
        in_specs=(tokens,) * 4 + (P(),),
        out_specs=(tokens,) * 4,
        check_vma=False,
    )
```

```python
import math

import jax
import jax.numpy as jnp
from jax import lax
from jax.experimental import pallas as pl
from jax.experimental.pallas import tpu as pltpu
from jax.sharding import PartitionSpec as P

HD = 128
HEADS = 24
FT = 512
FRAMES = 16
SUB = 16
OWNERS = 32
PLANES = 8
PER_PLANE = 3
UNITS = 8
SCALE = 1.0 / math.sqrt(HD)
EXP2 = SCALE * math.log2(math.e)
BF = jnp.bfloat16
F32 = jnp.float32
VMEM_MB = 60
GROUPS = ((0, 1), (1, 1), (2, 2))


def seat(pair, frame):
    return (frame >> 2) * 16 + pair * 4 + (frame & 1) * 2 + ((frame >> 1) & 1)


def shift_of(rel):
    return (1 - 2 * (rel & 1)) * lax.shift_left(jnp.int32(1), rel >> 1)


def inside(frame):
    return (frame >= 0) & (frame < FRAMES)


def crosses(frame, there, rel):
    return (rel < 4) & ((frame >> 2) != (there >> 2))


def sent_to(frame, rel):
    there = jnp.where(rel == 6, (frame + 8) & 15, frame + shift_of(rel))
    return there, inside(there) & jnp.logical_not(crosses(frame, there, rel))


def came_from(frame, rel):
    there = jnp.where(rel == 6, (frame + 8) & 15, frame - shift_of(rel))
    return there, inside(there)


def attention_kernel(
    q_in, k_in, v_in, g_in, mask,
    results,
    rows, kv, qg, scores, gradw, weights, scores_b, parts, back, onway, outs,
    peak, acc, dq_acc, rowl, rowd, qt, gt, bias,
    in_sem, s1, r1, s2, r2, s3, r3, s4, r4, s5, r6,
):
    seq = lax.axis_index("seq")
    plane = lax.axis_index("head")
    src_frame = seq >> 2
    src_spot = (seq & 3) * 8 + plane
    frame = (seq >> 4) * 4 + (seq & 1) * 2 + ((seq >> 1) & 1)
    pair = (seq >> 2) & 3
    within = (pair - plane) & 3
    busy = within < PER_PLANE
    head = plane * PER_PLANE + within
    own_hit = busy & (frame == src_frame)
    my_head = jnp.where(own_hit, head, -1)
    my_spot = jnp.where(own_hit, src_spot, -1)
    seat0 = seat(0, src_frame)
    row, col = frame >> 2, frame & 3
    low = col < 2
    hub = jnp.where(low, 5, 4)
    has_hub = jnp.where(low, row < 3, row > 0)

    def passed_to(gap):
        there = row * 4 + jnp.where(low, 4 + col - gap, col - 4 + gap)
        ok = has_hub & ((there >> 2) == row)
        return there, ok, 2 * (gap - 1) + low.astype(jnp.int32)


    fetch = [
        pltpu.make_async_copy(ref, rows.at[n], in_sem.at[n])
        for n, ref in enumerate((k_in, v_in, q_in, g_in))
    ]
    for copy in fetch:
        copy.start()

    barrier = pltpu.get_barrier_semaphore()

    def greet(target):
        pl.semaphore_signal(
            barrier, inc=1, device_id=target, device_id_type=pl.DeviceIdType.MESH
        )

    @pl.when(busy)
    def _():
        def greet_owners(z, carry):
            for r in range(4):
                greet((frame * 4 + r, z))

            return carry

        lax.fori_loop(0, PLANES, greet_owners, 0)

        for step in range(1, 4):
            greet((seat(pair, row * 4 + ((col + step) & 3)), plane))
        for rel in range(4, UNITS - 1):
            there, ok = sent_to(frame, jnp.int32(rel))

            @pl.when(ok)
            def _(there=there):
                greet((seat(pair, there), plane))

    partners = 4 + (row > 0).astype(jnp.int32) + (row < 3).astype(jnp.int32)
    expected = HEADS + busy.astype(jnp.int32) * partners
    for copy in fetch:
        copy.wait()
    pl.semaphore_wait(barrier, expected)

    def scatter(stage, dst):
        to = dst.at[:, pl.ds(pl.multiple_of(src_spot * SUB, SUB), SUB), :]

        def send(k, carry):
            off = 4 + ((k + 1) >> 1) * (2 * (k & 1) - 1)
            z = (plane + off) & 7
            for c in range(PER_PLANE):
                to_head = z * PER_PLANE + c
                src = rows.at[
                    pl.ds(2 * stage, 2), :, pl.ds(pl.multiple_of(to_head * HD, HD), HD)
                ]
                mine = to_head == my_head

                @pl.when(mine)
                def _(src=src):
                    pltpu.make_async_copy(src, to, r1.at[stage]).start()

                @pl.when(jnp.logical_not(mine))
                def _(src=src, c=c):
                    pltpu.make_async_remote_copy(
                        src_ref=src, dst_ref=to, send_sem=s1.at[stage], recv_sem=r1.at[stage],
                        device_id=(seat0 + ((c + z) & 3) * 4, z),
                        device_id_type=pl.DeviceIdType.MESH,
                    ).start()

            return carry

        lax.fori_loop(0, PLANES, send, 0)

    def wait_for(ref, sem):
        pltpu.make_async_copy(ref, ref, sem).wait()

    scatter(0, kv.at[0])
    scatter(1, qg)

    def kv_copy(rel):
        there, ok = sent_to(frame, rel)
        copy = pltpu.make_async_remote_copy(
            src_ref=kv.at[0], dst_ref=kv.at[rel + 1], send_sem=s2.at[rel], recv_sem=r2.at[rel],
            device_id=(seat(pair, there), plane), device_id_type=pl.DeviceIdType.MESH,
        )
        return copy, ok

    def pass_on(gap):
        there, ok, slot = passed_to(gap)
        copy = pltpu.make_async_remote_copy(
            src_ref=kv.at[hub + 1], dst_ref=kv.at[slot + 1], send_sem=s5.at[gap - 1],
            recv_sem=r2.at[slot],
            device_id=(seat(pair, there), plane), device_id_type=pl.DeviceIdType.MESH,
        )
        return copy, ok

    def grad_start(rel):
        there, _ = came_from(frame, rel)
        via = crosses(frame, there, rel)

        @pl.when(via)
        def _():
            pltpu.make_async_remote_copy(
                src_ref=parts.at[rel + 1], dst_ref=onway.at[rel >> 1], send_sem=s3.at[rel],
                recv_sem=r6.at[rel >> 1],
                device_id=(seat(pair, row * 4 + (there & 3)), plane),
                device_id_type=pl.DeviceIdType.MESH,
            ).start()

        @pl.when(jnp.logical_not(via))
        def _():
            pltpu.make_async_remote_copy(
                src_ref=parts.at[rel + 1], dst_ref=back.at[rel], send_sem=s3.at[rel],
                recv_sem=r3.at[rel],
                device_id=(seat(pair, there), plane), device_id_type=pl.DeviceIdType.MESH,
            ).start()

    def give_result(first, count, sem):
        arrays = pl.ds(first, count)
        dst = results.at[arrays, :, pl.ds(pl.multiple_of(head * HD, HD), HD)]

        def send(k, carry):
            z = (plane + 4 + ((k + 1) >> 1) * (2 * (k & 1) - 1)) & 7
            for r in range(4):
                spot = r * 8 + z
                src = outs.at[arrays, pl.ds(pl.multiple_of(spot * SUB, SUB), SUB), :]
                mine = spot == my_spot

                @pl.when(mine)
                def _(src=src):
                    pltpu.make_async_copy(src, dst, r4.at[sem]).start()

                @pl.when(jnp.logical_not(mine))
                def _(src=src, r=r):
                    pltpu.make_async_remote_copy(
                        src_ref=src, dst_ref=dst, send_sem=s4.at[sem], recv_sem=r4.at[sem],
                        device_id=(frame * 4 + r, z), device_id_type=pl.DeviceIdType.MESH,
                    ).start()

            return carry

        lax.fori_loop(0, PLANES, send, 0)

    @pl.when(busy)
    def _():
        pltpu.make_async_copy(kv.at[0], kv.at[0], r1.at[0]).wait()

        def send_partner(n, carry):
            rel = jnp.where(n < 2, n + 4, jnp.where(n < 6, n - 2, 6))
            copy, ok = kv_copy(rel)

            @pl.when(ok)
            def _():
                copy.start()

            return carry

        lax.fori_loop(0, UNITS - 1, send_partner, 0)

        lane_block = lax.broadcasted_iota(jnp.int32, (8, FT), 1) // 128
        bias[16] = jnp.zeros((8, FT), F32)

        def bias_row(n, carry):
            row = jnp.zeros((8, FT), F32)
            for kb in range(4):
                seen = mask[n // 4, n % 4, kb] > 0
                row = jnp.where(
                    (lane_block == kb) & jnp.logical_not(seen), jnp.float32(-jnp.inf), row
                )
            bias[n] = row
            return carry

        lax.fori_loop(0, 16, bias_row, 0)
        peak[...] = jnp.full((FT, HD), -jnp.inf, F32)
        acc[...] = jnp.zeros((FT, HD), F32)
        dq_acc[...] = jnp.zeros((FT, HD), F32)
        rowl[...] = jnp.zeros((FT, HD), F32)

        pltpu.make_async_copy(qg, qg, r1.at[1]).wait()
        qt[...] = qg[0].T

        def has_unit(u):
            return (u == 0) | came_from(frame, u - 1 + (u == 0).astype(jnp.int32))[1]

        def first_pass(n, carry):
            u = jnp.where(n == 0, 0, jnp.where(n < 3, n + 4, jnp.where(n < 7, n - 2, 7)))

            @pl.when(has_unit(u))
            def _():
                @pl.when(u > 0)
                def _():
                    wait_for(kv.at[u], r2.at[u - 1])

                @pl.when(u == hub + 1)
                def _():
                    for gap in (1, 2):
                        copy, ok = pass_on(gap)

                        @pl.when(ok)
                        def _(copy=copy):
                            copy.start()

                keys = kv[u, 0]
                values = kv[u, 1]
                for qb in range(4):
                    band = pl.ds(qb * 128, 128)
                    which = jnp.where(u == 0, 16, ((u + 1) // 2 - 1) * 4 + qb)
                    s = lax.dot_general(
                        qg[0, band], keys, (((1,), (1,)), ((), ())), preferred_element_type=F32
                    )
                    s = s + bias[which, 0:1, :]
                    scores[u, band] = s
                    top = jnp.maximum(
                        jnp.maximum(s[:, 0:128], s[:, 128:256]),
                        jnp.maximum(s[:, 256:384], s[:, 384:512]),
                    )
                    peak[band] = jnp.maximum(peak[band], top)
                    gradw[u, band] = lax.dot_general(
                        qg[1, band], values, (((1,), (1,)), ((), ())), preferred_element_type=F32
                    )

            return carry

        lax.fori_loop(0, UNITS, first_pass, 0)
        top = jnp.max(peak[...], axis=1, keepdims=True) * EXP2
        peak[...] = jnp.broadcast_to(top, (FT, HD))

        def second_pass(u, carry):
            @pl.when(has_unit(u))
            def _():
                for qb in range(4):
                    band = pl.ds(qb * 128, 128)
                    e = jnp.exp2(scores[u, band] * EXP2 - peak[band, 0:1])
                    rowl[band] += (e[:, 0:128] + e[:, 128:256]) + (e[:, 256:384] + e[:, 384:512])
                    weights[u, band] = e.astype(BF)
                acc[...] += jnp.dot(weights[u], kv[u, 1], preferred_element_type=F32)

            return carry

        lax.fori_loop(0, UNITS, second_pass, 0)
        inv = 1.0 / jnp.sum(rowl[...], axis=1, keepdims=True)
        attended = (acc[...] * inv).astype(BF)
        outs[0] = attended
        give_result(0, 1, 0)
        grads = qg[1].astype(F32)
        delta = jnp.sum(grads * attended.astype(F32), axis=1, keepdims=True)
        gt[...] = (grads * inv).astype(BF).T
        inv = inv * SCALE
        rowl[...] = jnp.broadcast_to(inv, (FT, HD))
        rowd[...] = jnp.broadcast_to(inv * delta, (FT, HD))

        def third_pass(n, carry):
            near = jnp.where(low, 1, 2)
            u = jnp.where(
                n < 2, near + 2 * n,
                jnp.where(
                    n == 2, 7,
                    jnp.where(
                        n == 3, 10 - hub,
                        jnp.where(n == 4, hub + 1, jnp.where(n < 7, 3 - near + 2 * (n - 5), 0)),
                    ),
                ),
            )

            @pl.when(has_unit(u))
            def _():
                for qb in range(4):
                    band = pl.ds(qb * 128, 128)
                    ds = weights[u, band].astype(F32) * (
                        gradw[u, band] * rowl[band, 0:1] - rowd[band, 0:1]
                    )
                    scores_b[u, band] = ds.astype(BF)
                ds = scores_b[u]
                parts[u, 0] = jnp.dot(qt[...], ds, preferred_element_type=F32).astype(BF)
                parts[u, 1] = jnp.dot(gt[...], weights[u], preferred_element_type=F32).astype(BF)

                @pl.when(u == hub + 1)
                def _():
                    for gap in (1, 2):

                        @pl.when(passed_to(gap)[1])
                        def _(gap=gap):
                            wait_for(onway.at[gap - 1], r6.at[gap - 1])
                            for n in range(2):
                                parts[u, n] = (
                                    parts[u, n].astype(F32) + onway[gap - 1, n].astype(F32)
                                ).astype(BF)

                @pl.when(u > 0)
                def _():
                    grad_start(u - 1)

                dq_acc[...] += jnp.dot(ds, kv[u, 0], preferred_element_type=F32)

            return carry

        lax.fori_loop(0, UNITS, third_pass, 0)
        outs[1] = dq_acc[...].astype(BF)
        give_result(1, 1, 1)

        sums = scores.at[0, pl.ds(0, 256)]
        sums[0:128] = parts[0, 0].astype(F32)
        sums[128:256] = parts[0, 1].astype(F32)

        def add_back(rel, carry):
            @pl.when(sent_to(frame, rel)[1])
            def _():
                pltpu.make_async_copy(back.at[rel], back.at[rel], r3.at[rel]).wait()
                sums[0:128] += back[rel, 0].astype(F32)
                sums[128:256] += back[rel, 1].astype(F32)

            return carry

        lax.fori_loop(0, UNITS - 1, add_back, 0)
        outs[2] = sums[0:128].T.astype(BF)
        outs[3] = sums[128:256].T.astype(BF)
        give_result(2, 2, 2)

        def partner_sent(rel, carry):
            copy, ok = kv_copy(rel)

            @pl.when(ok)
            def _():
                copy.wait_send()

            @pl.when(came_from(frame, rel)[1])
            def _():
                wait_for(parts.at[rel + 1], s3.at[rel])

            return carry

        lax.fori_loop(0, UNITS - 1, partner_sent, 0)
        for gap in (1, 2):
            copy, ok = pass_on(gap)

            @pl.when(ok)
            def _(copy=copy):
                copy.wait_send()

        for sem, (first, count) in enumerate(GROUPS):
            given = outs.at[pl.ds(first, count)]

            @pl.when(own_hit)
            def _(given=given, sem=sem):
                wait_for(given.at[:, pl.ds(0, FT - SUB)], s4.at[sem])

            @pl.when(jnp.logical_not(own_hit))
            def _(given=given, sem=sem):
                wait_for(given, s4.at[sem])

    for stage in range(2):
        sent = rows.at[pl.ds(2 * stage, 2)]

        @pl.when(own_hit)
        def _(sent=sent, stage=stage):
            wait_for(sent.at[:, :, pl.ds(0, (HEADS - 1) * HD)], s1.at[stage])

        @pl.when(jnp.logical_not(own_hit))
        def _(sent=sent, stage=stage):
            wait_for(sent, s1.at[stage])

    for sem, (first, count) in enumerate(GROUPS):
        wait_for(results.at[pl.ds(first, count)], r4.at[sem])


def per_device(query_rows, key_rows, value_rows, out_grad, block_mask):
    anywhere = pl.BlockSpec(memory_space=pl.ANY)
    result = jax.ShapeDtypeStruct(query_rows.shape, BF)
    dma = pltpu.SemaphoreType.DMA
    results = pl.pallas_call(
        attention_kernel,
        out_shape=jax.ShapeDtypeStruct((4,) + query_rows.shape, BF),
        in_specs=[anywhere] * 4 + [pl.BlockSpec(memory_space=pltpu.SMEM)],
        out_specs=anywhere,
        scratch_shapes=[
            pltpu.VMEM((4, SUB, HEADS * HD), BF),
            pltpu.VMEM((UNITS, 2, FT, HD), BF),
            pltpu.VMEM((2, FT, HD), BF),
            pltpu.VMEM((UNITS, FT, FT), F32),
            pltpu.VMEM((UNITS, FT, FT), F32),
            pltpu.VMEM((UNITS, FT, FT), BF),
            pltpu.VMEM((UNITS, FT, FT), BF),
            pltpu.VMEM((UNITS, 2, HD, FT), BF),
            pltpu.VMEM((UNITS - 1, 2, HD, FT), BF),
            pltpu.VMEM((2, 2, HD, FT), BF),
            pltpu.VMEM((4, FT, HD), BF),
            pltpu.VMEM((FT, HD), F32),
            pltpu.VMEM((FT, HD), F32),
            pltpu.VMEM((FT, HD), F32),
            pltpu.VMEM((FT, HD), F32),
            pltpu.VMEM((FT, HD), F32),
            pltpu.VMEM((HD, FT), BF),
            pltpu.VMEM((HD, FT), BF),
            pltpu.VMEM((17, 8, FT), F32),
            dma((4,)),
            dma((2,)),
            dma((2,)),
            dma((UNITS - 1,)),
            dma((UNITS - 1,)),
            dma((UNITS - 1,)),
            dma((UNITS - 1,)),
            dma((3,)),
            dma((3,)),
            dma((2,)),
            dma((2,)),
        ],
        compiler_params=pltpu.CompilerParams(
            collective_id=0, has_side_effects=True, vmem_limit_bytes=VMEM_MB * 1024 * 1024
        ),
    )(query_rows, key_rows, value_rows, out_grad, block_mask)
    return tuple(results[n] for n in range(4))


def solution(mesh):
    tokens = P(("seq", "head"), None)
    return jax.shard_map(
        per_device,
        mesh=mesh,
        in_specs=(tokens,) * 4 + (P(),),
        out_specs=(tokens,) * 4,
        check_vma=False,
    )
```

```python
import math

import jax
import jax.numpy as jnp
from jax import lax
from jax.experimental import pallas as pl
from jax.experimental.pallas import tpu as pltpu
from jax.sharding import PartitionSpec as P

HD = 128
HEADS = 24
FT = 512
FRAMES = 16
SUB = 16
OWNERS = 32
PLANES = 8
PER_PLANE = 3
UNITS = 8
SCALE = 1.0 / math.sqrt(HD)
EXP2 = SCALE * math.log2(math.e)
BF = jnp.bfloat16
F32 = jnp.float32
VMEM_MB = 60
GROUPS = ((0, 1), (1, 1), (2, 2))


def seat(pair, frame):
    return (frame >> 2) * 16 + pair * 4 + (frame & 1) * 2 + ((frame >> 1) & 1)


def shift_of(rel):
    return (1 - 2 * (rel & 1)) * lax.shift_left(jnp.int32(1), rel >> 1)


def order(steps, n):
    return lax.shift_right_logical(
        jnp.int32(sum(step << (3 * k) for k, step in enumerate(steps))), 3 * n
    ) & 7


def inside(frame):
    return (frame >= 0) & (frame < FRAMES)


def crosses(frame, there, rel):
    return (rel < 4) & ((frame >> 2) != (there >> 2))


def sent_to(frame, rel):
    there = jnp.where(rel == 6, (frame + 8) & 15, frame + shift_of(rel))
    return there, inside(there) & jnp.logical_not(crosses(frame, there, rel))


def came_from(frame, rel):
    there = jnp.where(rel == 6, (frame + 8) & 15, frame - shift_of(rel))
    return there, inside(there)


def attention_kernel(
    q_in, k_in, v_in, g_in, mask,
    results,
    rows, kv, qg, scores, gradw, weights, scores_b, parts, back, onway, outs,
    peak, acc, dq_acc, rowl, rowd, qt, gt, bias,
    in_sem, s1, r1, s2, r2, s3, r3, s4, r4, s5, r6,
):
    seq = lax.axis_index("seq")
    plane = lax.axis_index("head")
    src_frame = seq >> 2
    src_spot = (seq & 3) * 8 + plane
    frame = (seq >> 4) * 4 + (seq & 1) * 2 + ((seq >> 1) & 1)
    pair = (seq >> 2) & 3
    within = (pair - plane) & 3
    busy = within < PER_PLANE
    head = plane * PER_PLANE + within
    own_hit = busy & (frame == src_frame)
    my_head = jnp.where(own_hit, head, -1)
    my_spot = jnp.where(own_hit, src_spot, -1)
    seat0 = seat(0, src_frame)
    row, col = frame >> 2, frame & 3
    low = col < 2
    hub = jnp.where(low, 5, 4)
    has_hub = jnp.where(low, row < 3, row > 0)

    def passed_to(gap):
        there = row * 4 + jnp.where(low, 4 + col - gap, col - 4 + gap)
        ok = has_hub & ((there >> 2) == row)
        return there, ok, 2 * (gap - 1) + low.astype(jnp.int32)


    fetch = [
        pltpu.make_async_copy(ref, rows.at[n], in_sem.at[n])
        for n, ref in enumerate((k_in, v_in, q_in, g_in))
    ]
    for copy in fetch:
        copy.start()

    barrier = pltpu.get_barrier_semaphore()

    def greet(target):
        pl.semaphore_signal(
            barrier, inc=1, device_id=target, device_id_type=pl.DeviceIdType.MESH
        )

    @pl.when(busy)
    def _():
        def greet_owners(z, carry):
            for r in range(4):
                greet((frame * 4 + r, z))

            return carry

        lax.fori_loop(0, PLANES, greet_owners, 0)

        for step in range(1, 4):
            greet((seat(pair, row * 4 + ((col + step) & 3)), plane))
        for rel in range(4, UNITS - 1):
            there, ok = sent_to(frame, jnp.int32(rel))

            @pl.when(ok)
            def _(there=there):
                greet((seat(pair, there), plane))

    partners = 4 + (row > 0).astype(jnp.int32) + (row < 3).astype(jnp.int32)
    expected = HEADS + busy.astype(jnp.int32) * partners
    for copy in fetch:
        copy.wait()
    pl.semaphore_wait(barrier, expected)

    def scatter(stage, dst):
        to = dst.at[:, pl.ds(pl.multiple_of(src_spot * SUB, SUB), SUB), :]

        def send(k, carry):
            off = 4 + ((k + 1) >> 1) * (2 * (k & 1) - 1)
            z = (plane + off) & 7
            for c in range(PER_PLANE):
                to_head = z * PER_PLANE + c
                src = rows.at[
                    pl.ds(2 * stage, 2), :, pl.ds(pl.multiple_of(to_head * HD, HD), HD)
                ]
                mine = to_head == my_head

                @pl.when(mine)
                def _(src=src):
                    pltpu.make_async_copy(src, to, r1.at[stage]).start()

                @pl.when(jnp.logical_not(mine))
                def _(src=src, c=c):
                    pltpu.make_async_remote_copy(
                        src_ref=src, dst_ref=to, send_sem=s1.at[stage], recv_sem=r1.at[stage],
                        device_id=(seat0 + ((c + z) & 3) * 4, z),
                        device_id_type=pl.DeviceIdType.MESH,
                    ).start()

            return carry

        lax.fori_loop(0, PLANES, send, 0)

    def wait_for(ref, sem):
        pltpu.make_async_copy(ref, ref, sem).wait()

    scatter(0, kv.at[0])
    scatter(1, qg)

    def kv_copy(rel):
        there, ok = sent_to(frame, rel)
        copy = pltpu.make_async_remote_copy(
            src_ref=kv.at[0], dst_ref=kv.at[rel + 1], send_sem=s2.at[rel], recv_sem=r2.at[rel],
            device_id=(seat(pair, there), plane), device_id_type=pl.DeviceIdType.MESH,
        )
        return copy, ok

    def pass_on(gap):
        there, ok, slot = passed_to(gap)
        copy = pltpu.make_async_remote_copy(
            src_ref=kv.at[hub + 1], dst_ref=kv.at[slot + 1], send_sem=s5.at[gap - 1],
            recv_sem=r2.at[slot],
            device_id=(seat(pair, there), plane), device_id_type=pl.DeviceIdType.MESH,
        )
        return copy, ok

    def share():
        return pltpu.make_async_remote_copy(
            src_ref=kv.at[2], dst_ref=kv.at[1], send_sem=s5.at[2], recv_sem=r2.at[0],
            device_id=(seat(pair, frame + 2), plane), device_id_type=pl.DeviceIdType.MESH,
        )

    def grad_start(rel):
        there, _ = came_from(frame, rel)
        via = crosses(frame, there, rel)
        spot = rel >> 1

        @pl.when(via)
        def _():
            pltpu.make_async_remote_copy(
                src_ref=parts.at[rel + 1], dst_ref=onway.at[spot], send_sem=s3.at[rel],
                recv_sem=r6.at[spot],
                device_id=(seat(pair, row * 4 + (there & 3)), plane),
                device_id_type=pl.DeviceIdType.MESH,
            ).start()

        @pl.when(jnp.logical_not(via))
        def _():
            pltpu.make_async_remote_copy(
                src_ref=parts.at[rel + 1], dst_ref=back.at[rel], send_sem=s3.at[rel],
                recv_sem=r3.at[rel],
                device_id=(seat(pair, there), plane), device_id_type=pl.DeviceIdType.MESH,
            ).start()

    def give_result(first, count, sem):
        arrays = pl.ds(first, count)
        dst = results.at[arrays, :, pl.ds(pl.multiple_of(head * HD, HD), HD)]

        def send(z, carry):
            for r in range(4):
                spot = r * 8 + z
                src = outs.at[arrays, pl.ds(pl.multiple_of(spot * SUB, SUB), SUB), :]
                mine = spot == my_spot

                @pl.when(mine)
                def _(src=src):
                    pltpu.make_async_copy(src, dst, r4.at[sem]).start()

                @pl.when(jnp.logical_not(mine))
                def _(src=src, r=r):
                    pltpu.make_async_remote_copy(
                        src_ref=src, dst_ref=dst, send_sem=s4.at[sem], recv_sem=r4.at[sem],
                        device_id=(frame * 4 + r, z), device_id_type=pl.DeviceIdType.MESH,
                    ).start()

            return carry

        lax.fori_loop(0, PLANES, send, 0)

    @pl.when(busy)
    def _():
        pltpu.make_async_copy(kv.at[0], kv.at[0], r1.at[0]).wait()

        def send_partner(n, carry):
            rel = order((4, 5, 1, 0, 2, 3, 6), n)
            copy, ok = kv_copy(rel)

            @pl.when(ok & ((rel > 0) | (col == 0)))
            def _():
                copy.start()

            return carry

        lax.fori_loop(0, UNITS - 1, send_partner, 0)

        lane_block = lax.broadcasted_iota(jnp.int32, (8, FT), 1) // 128
        bias[16] = jnp.zeros((8, FT), F32)

        def bias_row(n, carry):
            row = jnp.zeros((8, FT), F32)
            for kb in range(4):
                seen = mask[n // 4, n % 4, kb] > 0
                row = jnp.where(
                    (lane_block == kb) & jnp.logical_not(seen), jnp.float32(-jnp.inf), row
                )
            bias[n] = row
            return carry

        lax.fori_loop(0, 16, bias_row, 0)
        peak[...] = jnp.full((FT, HD), -jnp.inf, F32)
        acc[...] = jnp.zeros((FT, HD), F32)
        dq_acc[...] = jnp.zeros((FT, HD), F32)
        rowl[...] = jnp.zeros((FT, HD), F32)

        pltpu.make_async_copy(qg, qg, r1.at[1]).wait()
        qt[...] = qg[0].T

        def has_unit(u):
            return (u == 0) | came_from(frame, u - 1 + (u == 0).astype(jnp.int32))[1]

        def first_pass(n, carry):
            u = jnp.where(
                low, order((0, 6, 2, 5, 1, 3, 4, 7), n), order((0, 5, 6, 2, 3, 4, 1, 7), n)
            )

            @pl.when(has_unit(u))
            def _():
                @pl.when(u > 0)
                def _():
                    wait_for(kv.at[u], r2.at[u - 1])

                @pl.when(low & (u == 2))
                def _():
                    share().start()

                @pl.when(u == hub + 1)
                def _():
                    for gap in (1, 2):
                        copy, ok = pass_on(gap)

                        @pl.when(ok)
                        def _(copy=copy):
                            copy.start()

                keys = kv[u, 0]
                values = kv[u, 1]
                for qb in range(4):
                    band = pl.ds(qb * 128, 128)
                    which = jnp.where(u == 0, 16, ((u + 1) // 2 - 1) * 4 + qb)
                    s = lax.dot_general(
                        qg[0, band], keys, (((1,), (1,)), ((), ())), preferred_element_type=F32
                    )
                    s = s + bias[which, 0:1, :]
                    scores[u, band] = s
                    top = jnp.maximum(
                        jnp.maximum(s[:, 0:128], s[:, 128:256]),
                        jnp.maximum(s[:, 256:384], s[:, 384:512]),
                    )
                    peak[band] = jnp.maximum(peak[band], top)
                    gradw[u, band] = lax.dot_general(
                        qg[1, band], values, (((1,), (1,)), ((), ())), preferred_element_type=F32
                    )

            return carry

        lax.fori_loop(0, UNITS, first_pass, 0)
        top = jnp.max(peak[...], axis=1, keepdims=True) * EXP2
        peak[...] = jnp.broadcast_to(top, (FT, HD))

        def second_pass(u, carry):
            @pl.when(has_unit(u))
            def _():
                for qb in range(4):
                    band = pl.ds(qb * 128, 128)
                    e = jnp.exp2(scores[u, band] * EXP2 - peak[band, 0:1])
                    rowl[band] += (e[:, 0:128] + e[:, 128:256]) + (e[:, 256:384] + e[:, 384:512])
                    weights[u, band] = e.astype(BF)
                acc[...] += jnp.dot(weights[u], kv[u, 1], preferred_element_type=F32)

            return carry

        lax.fori_loop(0, UNITS, second_pass, 0)
        inv = 1.0 / jnp.sum(rowl[...], axis=1, keepdims=True)
        attended = (acc[...] * inv).astype(BF)
        outs[0] = attended
        give_result(0, 1, 0)
        grads = qg[1].astype(F32)
        delta = jnp.sum(grads * attended.astype(F32), axis=1, keepdims=True)
        gt[...] = (grads * inv).astype(BF).T
        inv = inv * SCALE
        rowl[...] = jnp.broadcast_to(inv, (FT, HD))
        rowd[...] = jnp.broadcast_to(inv * delta, (FT, HD))

        def collect(u, spot):
            wait_for(onway.at[spot], r6.at[spot])
            for n in range(2):
                parts[u, n] = (parts[u, n].astype(F32) + onway[spot, n].astype(F32)).astype(BF)

        def third_pass(n, carry):
            u = jnp.where(
                low, order((1, 3, 7, 5, 6, 2, 4, 0), n), order((2, 4, 7, 6, 5, 1, 3, 0), n)
            )

            @pl.when(has_unit(u))
            def _():
                for qb in range(4):
                    band = pl.ds(qb * 128, 128)
                    ds = weights[u, band].astype(F32) * (
                        gradw[u, band] * rowl[band, 0:1] - rowd[band, 0:1]
                    )
                    scores_b[u, band] = ds.astype(BF)
                ds = scores_b[u]
                parts[u, 0] = jnp.dot(qt[...], ds, preferred_element_type=F32).astype(BF)
                parts[u, 1] = jnp.dot(gt[...], weights[u], preferred_element_type=F32).astype(BF)

                @pl.when(u == hub + 1)
                def _():
                    for gap in (1, 2):

                        @pl.when(passed_to(gap)[1])
                        def _(gap=gap):
                            collect(u, gap - 1)


                @pl.when(u > 0)
                def _():
                    grad_start(u - 1)

                dq_acc[...] += jnp.dot(ds, kv[u, 0], preferred_element_type=F32)

            return carry

        lax.fori_loop(0, UNITS, third_pass, 0)
        outs[1] = dq_acc[...].astype(BF)
        give_result(1, 1, 1)

        sums = scores.at[0, pl.ds(0, 256)]
        sums[0:128] = parts[0, 0].astype(F32)
        sums[128:256] = parts[0, 1].astype(F32)

        def add_back(rel, carry):
            @pl.when(sent_to(frame, rel)[1])
            def _():
                pltpu.make_async_copy(back.at[rel], back.at[rel], r3.at[rel]).wait()
                sums[0:128] += back[rel, 0].astype(F32)
                sums[128:256] += back[rel, 1].astype(F32)

            return carry

        lax.fori_loop(0, UNITS - 1, add_back, 0)
        outs[2] = sums[0:128].T.astype(BF)
        outs[3] = sums[128:256].T.astype(BF)
        give_result(2, 2, 2)

        def partner_sent(rel, carry):
            copy, ok = kv_copy(rel)

            @pl.when(ok & ((rel > 0) | (col == 0)))
            def _():
                copy.wait_send()

            @pl.when(came_from(frame, rel)[1])
            def _():
                wait_for(parts.at[rel + 1], s3.at[rel])

            return carry

        lax.fori_loop(0, UNITS - 1, partner_sent, 0)
        for gap in (1, 2):
            copy, ok = pass_on(gap)

            @pl.when(ok)
            def _(copy=copy):
                copy.wait_send()

        @pl.when(low)
        def _():
            share().wait_send()

        for sem, (first, count) in enumerate(GROUPS):
            given = outs.at[pl.ds(first, count)]

            @pl.when(own_hit)
            def _(given=given, sem=sem):
                wait_for(given.at[:, pl.ds(0, FT - SUB)], s4.at[sem])

            @pl.when(jnp.logical_not(own_hit))
            def _(given=given, sem=sem):
                wait_for(given, s4.at[sem])

    for stage in range(2):
        sent = rows.at[pl.ds(2 * stage, 2)]

        @pl.when(own_hit)
        def _(sent=sent, stage=stage):
            wait_for(sent.at[:, :, pl.ds(0, (HEADS - 1) * HD)], s1.at[stage])

        @pl.when(jnp.logical_not(own_hit))
        def _(sent=sent, stage=stage):
            wait_for(sent, s1.at[stage])

    for sem, (first, count) in enumerate(GROUPS):
        wait_for(results.at[pl.ds(first, count)], r4.at[sem])


def per_device(query_rows, key_rows, value_rows, out_grad, block_mask):
    anywhere = pl.BlockSpec(memory_space=pl.ANY)
    result = jax.ShapeDtypeStruct(query_rows.shape, BF)
    dma = pltpu.SemaphoreType.DMA
    results = pl.pallas_call(
        attention_kernel,
        out_shape=jax.ShapeDtypeStruct((4,) + query_rows.shape, BF),
        in_specs=[anywhere] * 4 + [pl.BlockSpec(memory_space=pltpu.SMEM)],
        out_specs=anywhere,
        scratch_shapes=[
            pltpu.VMEM((4, SUB, HEADS * HD), BF),
            pltpu.VMEM((UNITS, 2, FT, HD), BF),
            pltpu.VMEM((2, FT, HD), BF),
            pltpu.VMEM((UNITS, FT, FT), F32),
            pltpu.VMEM((UNITS, FT, FT), F32),
            pltpu.VMEM((UNITS, FT, FT), BF),
            pltpu.VMEM((UNITS, FT, FT), BF),
            pltpu.VMEM((UNITS, 2, HD, FT), BF),
            pltpu.VMEM((UNITS - 1, 2, HD, FT), BF),
            pltpu.VMEM((2, 2, HD, FT), BF),
            pltpu.VMEM((4, FT, HD), BF),
            pltpu.VMEM((FT, HD), F32),
            pltpu.VMEM((FT, HD), F32),
            pltpu.VMEM((FT, HD), F32),
            pltpu.VMEM((FT, HD), F32),
            pltpu.VMEM((FT, HD), F32),
            pltpu.VMEM((HD, FT), BF),
            pltpu.VMEM((HD, FT), BF),
            pltpu.VMEM((17, 8, FT), F32),
            dma((4,)),
            dma((2,)),
            dma((2,)),
            dma((UNITS - 1,)),
            dma((UNITS - 1,)),
            dma((UNITS - 1,)),
            dma((UNITS - 1,)),
            dma((3,)),
            dma((3,)),
            dma((3,)),
            dma((2,)),
        ],
        compiler_params=pltpu.CompilerParams(
            collective_id=0, has_side_effects=True, vmem_limit_bytes=VMEM_MB * 1024 * 1024
        ),
    )(query_rows, key_rows, value_rows, out_grad, block_mask)
    return tuple(results[n] for n in range(4))


def solution(mesh):
    tokens = P(("seq", "head"), None)
    return jax.shard_map(
        per_device,
        mesh=mesh,
        in_specs=(tokens,) * 4 + (P(),),
        out_specs=(tokens,) * 4,
        check_vma=False,
    )
```

```python
import math

import jax
import jax.numpy as jnp
from jax import lax
from jax.experimental import pallas as pl
from jax.experimental.pallas import tpu as pltpu
from jax.sharding import PartitionSpec as P

HD = 128
HEADS = 24
FT = 512
FRAMES = 16
SUB = 16
OWNERS = 32
PLANES = 8
PER_PLANE = 3
UNITS = 8
SCALE = 1.0 / math.sqrt(HD)
EXP2 = SCALE * math.log2(math.e)
BF = jnp.bfloat16
F32 = jnp.float32
VMEM_MB = 60
GROUPS = ((0, 1), (1, 1), (2, 2))


def seat(pair, frame):
    return (frame >> 2) * 16 + pair * 4 + (frame & 1) * 2 + ((frame >> 1) & 1)


def shift_of(rel):
    return (1 - 2 * (rel & 1)) * lax.shift_left(jnp.int32(1), rel >> 1)


def order(steps, n):
    return lax.shift_right_logical(
        jnp.int32(sum(step << (3 * k) for k, step in enumerate(steps))), 3 * n
    ) & 7


def inside(frame):
    return (frame >= 0) & (frame < FRAMES)


def crosses(frame, there, rel):
    return (rel < 4) & ((frame >> 2) != (there >> 2))


def sent_to(frame, rel):
    there = jnp.where(rel == 6, (frame + 8) & 15, frame + shift_of(rel))
    return there, inside(there) & jnp.logical_not(crosses(frame, there, rel))


def came_from(frame, rel):
    there = jnp.where(rel == 6, (frame + 8) & 15, frame - shift_of(rel))
    return there, inside(there)


def attention_kernel(
    q_in, k_in, v_in, g_in, mask,
    results,
    rows, kv, qg, scores, gradw, weights, scores_b, parts, back, onway, outs,
    peak, acc, dq_acc, rowl, rowd, qt, gt, bias,
    in_sem, s1, r1, s2, r2, s3, r3, s4, r4, s5, r6,
):
    seq = lax.axis_index("seq")
    plane = lax.axis_index("head")
    src_frame = seq >> 2
    src_spot = (seq & 3) * 8 + plane
    frame = (seq >> 4) * 4 + (seq & 1) * 2 + ((seq >> 1) & 1)
    pair = (seq >> 2) & 3
    within = (pair - plane) & 3
    busy = within < PER_PLANE
    head = plane * PER_PLANE + within
    own_hit = busy & (frame == src_frame)
    my_head = jnp.where(own_hit, head, -1)
    my_spot = jnp.where(own_hit, src_spot, -1)
    seat0 = seat(0, src_frame)
    row, col = frame >> 2, frame & 3
    low = col < 2
    hub = jnp.where(low, 5, 4)
    has_hub = jnp.where(low, row < 3, row > 0)

    def passed_to(gap):
        there = row * 4 + jnp.where(low, 4 + col - gap, col - 4 + gap)
        ok = has_hub & ((there >> 2) == row)
        return there, ok, 2 * (gap - 1) + low.astype(jnp.int32)


    fetch = [
        pltpu.make_async_copy(ref, rows.at[n], in_sem.at[n])
        for n, ref in enumerate((k_in, v_in, q_in, g_in))
    ]
    barrier = pltpu.get_barrier_semaphore()

    def greet(target):
        pl.semaphore_signal(
            barrier, inc=1, device_id=target, device_id_type=pl.DeviceIdType.MESH
        )

    @pl.when(busy)
    def _():
        def greet_owners(z, carry):
            for r in range(4):
                greet((frame * 4 + r, z))

            return carry

        lax.fori_loop(0, PLANES, greet_owners, 0)

        for step in range(1, 4):
            greet((seat(pair, row * 4 + ((col + step) & 3)), plane))
        for rel in range(4, UNITS - 1):
            there, ok = sent_to(frame, jnp.int32(rel))

            @pl.when(ok)
            def _(there=there):
                greet((seat(pair, there), plane))

    for copy in fetch:
        copy.start()

    partners = 4 + (row > 0).astype(jnp.int32) + (row < 3).astype(jnp.int32)
    expected = HEADS + busy.astype(jnp.int32) * partners
    for copy in fetch:
        copy.wait()
    pl.semaphore_wait(barrier, expected)

    def scatter(stage, dst):
        to = dst.at[:, pl.ds(pl.multiple_of(src_spot * SUB, SUB), SUB), :]

        def send(k, carry):
            off = 4 + ((k + 1) >> 1) * (2 * (k & 1) - 1)
            z = (plane + off) & 7
            for c in range(PER_PLANE):
                to_head = z * PER_PLANE + c
                src = rows.at[
                    pl.ds(2 * stage, 2), :, pl.ds(pl.multiple_of(to_head * HD, HD), HD)
                ]
                mine = to_head == my_head

                @pl.when(mine)
                def _(src=src):
                    pltpu.make_async_copy(src, to, r1.at[stage]).start()

                @pl.when(jnp.logical_not(mine))
                def _(src=src, c=c):
                    pltpu.make_async_remote_copy(
                        src_ref=src, dst_ref=to, send_sem=s1.at[stage], recv_sem=r1.at[stage],
                        device_id=(seat0 + ((c + z) & 3) * 4, z),
                        device_id_type=pl.DeviceIdType.MESH,
                    ).start()

            return carry

        lax.fori_loop(0, PLANES, send, 0)

    def wait_for(ref, sem):
        pltpu.make_async_copy(ref, ref, sem).wait()

    scatter(0, kv.at[0])
    scatter(1, qg)

    def kv_copy(rel):
        there, ok = sent_to(frame, rel)
        copy = pltpu.make_async_remote_copy(
            src_ref=kv.at[0], dst_ref=kv.at[rel + 1], send_sem=s2.at[rel], recv_sem=r2.at[rel],
            device_id=(seat(pair, there), plane), device_id_type=pl.DeviceIdType.MESH,
        )
        return copy, ok

    def pass_on(gap):
        there, ok, slot = passed_to(gap)
        copy = pltpu.make_async_remote_copy(
            src_ref=kv.at[hub + 1], dst_ref=kv.at[slot + 1], send_sem=s5.at[gap - 1],
            recv_sem=r2.at[slot],
            device_id=(seat(pair, there), plane), device_id_type=pl.DeviceIdType.MESH,
        )
        return copy, ok

    def share():
        return pltpu.make_async_remote_copy(
            src_ref=kv.at[2], dst_ref=kv.at[1], send_sem=s5.at[2], recv_sem=r2.at[0],
            device_id=(seat(pair, frame + 2), plane), device_id_type=pl.DeviceIdType.MESH,
        )

    def grad_start(rel):
        there, _ = came_from(frame, rel)
        via = crosses(frame, there, rel)
        spot = rel >> 1

        @pl.when(via)
        def _():
            pltpu.make_async_remote_copy(
                src_ref=parts.at[rel + 1], dst_ref=onway.at[spot], send_sem=s3.at[rel],
                recv_sem=r6.at[spot],
                device_id=(seat(pair, row * 4 + (there & 3)), plane),
                device_id_type=pl.DeviceIdType.MESH,
            ).start()

        @pl.when(jnp.logical_not(via))
        def _():
            pltpu.make_async_remote_copy(
                src_ref=parts.at[rel + 1], dst_ref=back.at[rel], send_sem=s3.at[rel],
                recv_sem=r3.at[rel],
                device_id=(seat(pair, there), plane), device_id_type=pl.DeviceIdType.MESH,
            ).start()

    def give_result(first, count, sem):
        arrays = pl.ds(first, count)
        dst = results.at[arrays, :, pl.ds(pl.multiple_of(head * HD, HD), HD)]

        def send(z, carry):
            for r in range(4):
                spot = r * 8 + z
                src = outs.at[arrays, pl.ds(pl.multiple_of(spot * SUB, SUB), SUB), :]
                mine = spot == my_spot

                @pl.when(mine)
                def _(src=src):
                    pltpu.make_async_copy(src, dst, r4.at[sem]).start()

                @pl.when(jnp.logical_not(mine))
                def _(src=src, r=r):
                    pltpu.make_async_remote_copy(
                        src_ref=src, dst_ref=dst, send_sem=s4.at[sem], recv_sem=r4.at[sem],
                        device_id=(frame * 4 + r, z), device_id_type=pl.DeviceIdType.MESH,
                    ).start()

            return carry

        lax.fori_loop(0, PLANES, send, 0)

    @pl.when(busy)
    def _():
        pltpu.make_async_copy(kv.at[0], kv.at[0], r1.at[0]).wait()

        def send_partner(n, carry):
            rel = order((4, 5, 1, 0, 2, 3, 6), n)
            copy, ok = kv_copy(rel)

            @pl.when(ok & ((rel > 0) | (col == 0)))
            def _():
                copy.start()

            return carry

        lax.fori_loop(0, UNITS - 1, send_partner, 0)

        lane_block = lax.broadcasted_iota(jnp.int32, (8, FT), 1) // 128
        bias[16] = jnp.zeros((8, FT), F32)

        def bias_row(n, carry):
            row = jnp.zeros((8, FT), F32)
            for kb in range(4):
                seen = mask[n // 4, n % 4, kb] > 0
                row = jnp.where(
                    (lane_block == kb) & jnp.logical_not(seen), jnp.float32(-jnp.inf), row
                )
            bias[n] = row
            return carry

        lax.fori_loop(0, 16, bias_row, 0)
        peak[...] = jnp.full((FT, HD), -jnp.inf, F32)
        acc[...] = jnp.zeros((FT, HD), F32)
        dq_acc[...] = jnp.zeros((FT, HD), F32)
        rowl[...] = jnp.zeros((FT, HD), F32)

        pltpu.make_async_copy(qg, qg, r1.at[1]).wait()
        qt[...] = qg[0].T

        def has_unit(u):
            return (u == 0) | came_from(frame, u - 1 + (u == 0).astype(jnp.int32))[1]

        def first_pass(n, carry):
            u = jnp.where(
                low, order((0, 6, 2, 5, 1, 3, 4, 7), n), order((0, 5, 6, 2, 3, 4, 1, 7), n)
            )

            @pl.when(has_unit(u))
            def _():
                @pl.when(u > 0)
                def _():
                    wait_for(kv.at[u], r2.at[u - 1])

                @pl.when(low & (u == 2))
                def _():
                    share().start()

                @pl.when(u == hub + 1)
                def _():
                    for gap in (1, 2):
                        copy, ok = pass_on(gap)

                        @pl.when(ok)
                        def _(copy=copy):
                            copy.start()

                keys = kv[u, 0]
                values = kv[u, 1]
                for qb in range(4):
                    band = pl.ds(qb * 128, 128)
                    which = jnp.where(u == 0, 16, ((u + 1) // 2 - 1) * 4 + qb)
                    s = lax.dot_general(
                        qg[0, band], keys, (((1,), (1,)), ((), ())), preferred_element_type=F32
                    )
                    s = s + bias[which, 0:1, :]
                    scores[u, band] = s
                    top = jnp.maximum(
                        jnp.maximum(s[:, 0:128], s[:, 128:256]),
                        jnp.maximum(s[:, 256:384], s[:, 384:512]),
                    )
                    peak[band] = jnp.maximum(peak[band], top)
                    gradw[u, band] = lax.dot_general(
                        qg[1, band], values, (((1,), (1,)), ((), ())), preferred_element_type=F32
                    )

            return carry

        lax.fori_loop(0, UNITS, first_pass, 0)
        top = jnp.max(peak[...], axis=1, keepdims=True) * EXP2
        peak[...] = jnp.broadcast_to(top, (FT, HD))

        def second_pass(u, carry):
            @pl.when(has_unit(u))
            def _():
                for qb in range(4):
                    band = pl.ds(qb * 128, 128)
                    e = jnp.exp2(scores[u, band] * EXP2 - peak[band, 0:1])
                    rowl[band] += (e[:, 0:128] + e[:, 128:256]) + (e[:, 256:384] + e[:, 384:512])
                    weights[u, band] = e.astype(BF)
                acc[...] += jnp.dot(weights[u], kv[u, 1], preferred_element_type=F32)

            return carry

        lax.fori_loop(0, UNITS, second_pass, 0)
        inv = 1.0 / jnp.sum(rowl[...], axis=1, keepdims=True)
        attended = (acc[...] * inv).astype(BF)
        outs[0] = attended
        give_result(0, 1, 0)
        grads = qg[1].astype(F32)
        delta = jnp.sum(grads * attended.astype(F32), axis=1, keepdims=True)
        gt[...] = (grads * inv).astype(BF).T
        inv = inv * SCALE
        rowl[...] = jnp.broadcast_to(inv, (FT, HD))
        rowd[...] = jnp.broadcast_to(inv * delta, (FT, HD))

        def collect(u, spot):
            wait_for(onway.at[spot], r6.at[spot])
            for n in range(2):
                parts[u, n] = (parts[u, n].astype(F32) + onway[spot, n].astype(F32)).astype(BF)

        def third_pass(n, carry):
            u = jnp.where(
                low, order((1, 3, 5, 7, 6, 2, 4, 0), n), order((2, 4, 6, 7, 5, 1, 3, 0), n)
            )

            @pl.when(has_unit(u))
            def _():
                for qb in range(4):
                    band = pl.ds(qb * 128, 128)
                    ds = weights[u, band].astype(F32) * (
                        gradw[u, band] * rowl[band, 0:1] - rowd[band, 0:1]
                    )
                    scores_b[u, band] = ds.astype(BF)
                ds = scores_b[u]
                parts[u, 0] = jnp.dot(qt[...], ds, preferred_element_type=F32).astype(BF)
                parts[u, 1] = jnp.dot(gt[...], weights[u], preferred_element_type=F32).astype(BF)

                @pl.when(u == hub + 1)
                def _():
                    for gap in (1, 2):

                        @pl.when(passed_to(gap)[1])
                        def _(gap=gap):
                            collect(u, gap - 1)


                @pl.when(u > 0)
                def _():
                    grad_start(u - 1)

                dq_acc[...] += jnp.dot(ds, kv[u, 0], preferred_element_type=F32)

            return carry

        lax.fori_loop(0, UNITS, third_pass, 0)
        outs[1] = dq_acc[...].astype(BF)
        give_result(1, 1, 1)

        sums = scores.at[0, pl.ds(0, 256)]
        sums[0:128] = parts[0, 0].astype(F32)
        sums[128:256] = parts[0, 1].astype(F32)

        def add_back(n, carry):
            rel = order((6, 0, 1, 2, 3, 4, 5), n)

            @pl.when(sent_to(frame, rel)[1])
            def _():
                pltpu.make_async_copy(back.at[rel], back.at[rel], r3.at[rel]).wait()
                sums[0:128] += back[rel, 0].astype(F32)
                sums[128:256] += back[rel, 1].astype(F32)

            return carry

        lax.fori_loop(0, UNITS - 1, add_back, 0)
        outs[2] = sums[0:128].T.astype(BF)
        outs[3] = sums[128:256].T.astype(BF)
        give_result(2, 2, 2)

        def partner_sent(rel, carry):
            copy, ok = kv_copy(rel)

            @pl.when(ok & ((rel > 0) | (col == 0)))
            def _():
                copy.wait_send()

            @pl.when(came_from(frame, rel)[1])
            def _():
                wait_for(parts.at[rel + 1], s3.at[rel])

            return carry

        lax.fori_loop(0, UNITS - 1, partner_sent, 0)
        for gap in (1, 2):
            copy, ok = pass_on(gap)

            @pl.when(ok)
            def _(copy=copy):
                copy.wait_send()

        @pl.when(low)
        def _():
            share().wait_send()

        for sem, (first, count) in enumerate(GROUPS):
            given = outs.at[pl.ds(first, count)]

            @pl.when(own_hit)
            def _(given=given, sem=sem):
                wait_for(given.at[:, pl.ds(0, FT - SUB)], s4.at[sem])

            @pl.when(jnp.logical_not(own_hit))
            def _(given=given, sem=sem):
                wait_for(given, s4.at[sem])

    for stage in range(2):
        sent = rows.at[pl.ds(2 * stage, 2)]

        @pl.when(own_hit)
        def _(sent=sent, stage=stage):
            wait_for(sent.at[:, :, pl.ds(0, (HEADS - 1) * HD)], s1.at[stage])

        @pl.when(jnp.logical_not(own_hit))
        def _(sent=sent, stage=stage):
            wait_for(sent, s1.at[stage])

    for sem, (first, count) in enumerate(GROUPS):
        wait_for(results.at[pl.ds(first, count)], r4.at[sem])


def per_device(query_rows, key_rows, value_rows, out_grad, block_mask):
    anywhere = pl.BlockSpec(memory_space=pl.ANY)
    result = jax.ShapeDtypeStruct(query_rows.shape, BF)
    dma = pltpu.SemaphoreType.DMA
    results = pl.pallas_call(
        attention_kernel,
        out_shape=jax.ShapeDtypeStruct((4,) + query_rows.shape, BF),
        in_specs=[anywhere] * 4 + [pl.BlockSpec(memory_space=pltpu.SMEM)],
        out_specs=anywhere,
        scratch_shapes=[
            pltpu.VMEM((4, SUB, HEADS * HD), BF),
            pltpu.VMEM((UNITS, 2, FT, HD), BF),
            pltpu.VMEM((2, FT, HD), BF),
            pltpu.VMEM((UNITS, FT, FT), F32),
            pltpu.VMEM((UNITS, FT, FT), F32),
            pltpu.VMEM((UNITS, FT, FT), BF),
            pltpu.VMEM((UNITS, FT, FT), BF),
            pltpu.VMEM((UNITS, 2, HD, FT), BF),
            pltpu.VMEM((UNITS - 1, 2, HD, FT), BF),
            pltpu.VMEM((2, 2, HD, FT), BF),
            pltpu.VMEM((4, FT, HD), BF),
            pltpu.VMEM((FT, HD), F32),
            pltpu.VMEM((FT, HD), F32),
            pltpu.VMEM((FT, HD), F32),
            pltpu.VMEM((FT, HD), F32),
            pltpu.VMEM((FT, HD), F32),
            pltpu.VMEM((HD, FT), BF),
            pltpu.VMEM((HD, FT), BF),
            pltpu.VMEM((17, 8, FT), F32),
            dma((4,)),
            dma((2,)),
            dma((2,)),
            dma((UNITS - 1,)),
            dma((UNITS - 1,)),
            dma((UNITS - 1,)),
            dma((UNITS - 1,)),
            dma((3,)),
            dma((3,)),
            dma((3,)),
            dma((2,)),
        ],
        compiler_params=pltpu.CompilerParams(
            collective_id=0, has_side_effects=True, vmem_limit_bytes=VMEM_MB * 1024 * 1024
        ),
    )(query_rows, key_rows, value_rows, out_grad, block_mask)
    return tuple(results[n] for n in range(4))


def solution(mesh):
    tokens = P(("seq", "head"), None)
    return jax.shard_map(
        per_device,
        mesh=mesh,
        in_specs=(tokens,) * 4 + (P(),),
        out_specs=(tokens,) * 4,
        check_vma=False,
    )
```
